32 devices in a mesh: rep: 4 (over x, core), fsdp: 4 (over z), tp: 2 (over y).
Axes of the slice: x: 2, y: 2, z: 4, core: 2. Of those that a mesh axis runs over, the one named last changes fastest.
Arguments:
- images: bfloat16 [32, 577, 1024], P(('rep', 'fsdp')), may hold values from -6 to 6
- ln1_gain: bfloat16 [1024], P('fsdp'), may hold values from 0.5 to 1.5
- ln1_bias: bfloat16 [1024], P('fsdp'), may hold values from -3 to 3
- w_qkv: bfloat16 [3, 1024, 1024], P(None, 'fsdp', 'tp'), may hold values from -1.5 to 1.5
- b_qv: bfloat16 [2, 1024], P(None, ('tp', 'fsdp')), may hold values from -3 to 3
- w_out: bfloat16 [1024, 1024], P('tp', 'fsdp'), may hold values from -0.5 to 0.5
- b_out: bfloat16 [1024], P('fsdp'), may hold values from -3 to 3
- ln2_gain: bfloat16 [1024], P('fsdp'), may hold values from 0.5 to 1.5
- ln2_bias: bfloat16 [1024], P('fsdp'), may hold values from -3 to 3
- w_fc1: bfloat16 [1024, 4096], P('fsdp', 'tp'), may hold values from -0.1875 to 0.1875
- b_fc1: bfloat16 [4096], P(('tp', 'fsdp')), may hold values from -3 to 3
- w_fc2: bfloat16 [4096, 1024], P('tp', 'fsdp'), may hold values from -0.09375 to 0.09375
- b_fc2: bfloat16 [1024], P('fsdp'), may hold values from -3 to 3
- cotangent: bfloat16 [32, 577, 1024], P(('rep', 'fsdp')), may hold values from -6 to 6
Outputs:
- block_output: float32 [32, 577, 1024], P(('rep', 'fsdp'))
- input_grad: float32 [32, 577, 1024], P(('rep', 'fsdp'))
- grad_ln1_gain: float32 [1024], P('fsdp')
- grad_ln1_bias: float32 [1024], P('fsdp')
- grad_w_qkv: float32 [3, 1024, 1024], P(None, 'fsdp', 'tp')
- grad_b_qv: float32 [2, 1024], P(None, ('tp', 'fsdp'))
- grad_w_out: float32 [1024, 1024], P('tp', 'fsdp')
- grad_b_out: float32 [1024], P('fsdp')
- grad_ln2_gain: float32 [1024], P('fsdp')
- grad_ln2_bias: float32 [1024], P('fsdp')
- grad_w_fc1: float32 [1024, 4096], P('fsdp', 'tp')
- grad_b_fc1: float32 [4096], P(('tp', 'fsdp'))
- grad_w_fc2: float32 [4096, 1024], P('tp', 'fsdp')
- grad_b_fc2: float32 [1024], P('fsdp')
The draws below stay inside these ranges and needn't reach their ends.
All inputs are finite; a program needn't handle non-finite values.
Results may differ from the reference program's by a relative error of at most 0.013.
The reference program's roundings to bfloat16 on the way (of `act1`, `probs_b`, `context`, `act2`, `hidden`, `grad_pre_b`, `grad_resid1_b` and `grad_context`) count: a program that leaves them out, or rounds other values in their place, can miss the bound.
Values may be sent and summed in bfloat16 or wider, within the bound.
No kernel may reach another device: no remote copies, remote signals or barrier semaphores. Data moves between devices by JAX's collectives and lax.ppermute only.
A program may use at most 256 MiB of HBM per device.

```python
import jax
import jax.numpy as jnp
from jax import lax

D = 1024
HEADS = 16
HD = 64
FF = 4096
SEQ = 577
IMAGES = 32


def draw_w_qkv(key, part):
    base = jax.random.truncated_normal(key, -4.0, 4.0, (3, D, D), jnp.float32) * D ** (-0.5)
    base = jnp.clip(base, -1.5, 1.5)
    return base.astype(jnp.bfloat16)


def block_scale(rng, shape, shards, least, high):
    loudness = 1.0
    for position, blocks in shards:
        heights = jax.random.uniform(jax.random.fold_in(jax.random.fold_in(rng, 6), position), (blocks,), jnp.float32, least / len(shards), high / len(shards))
        loudness = loudness * jnp.repeat(jnp.exp(heights), shape[position] // blocks).reshape((-1,) + (1,) * (len(shape) - 1 - position))
    return loudness


def gaussian(key, extent, scale, reach, pieces=(), dtype=jnp.bfloat16):
    factor_of = block_scale(key, extent, pieces, -0.22, 0.18) if pieces else 1.0
    drawn = jax.random.normal(key, extent, jnp.float32) * scale * factor_of
    return jnp.minimum(jnp.maximum(drawn, -reach), reach).astype(dtype)


def setup_inputs(seed: int = 0) -> dict:
    arg_keys = jax.random.split(jax.random.key(seed), 15)
    images = gaussian(arg_keys[0], (IMAGES, SEQ, D), 1.0, 6.0, ((0, 16),))
    ln1_gain = jnp.clip(1.0 + 0.1 * jax.random.normal(arg_keys[1], (D,), jnp.float32), 0.5, 1.5).astype(jnp.bfloat16)
    ln1_bias = gaussian(arg_keys[2], (D,), 0.5, 3.0, ((0, 4),))
    w_qkv = draw_w_qkv(jax.random.fold_in(arg_keys[14], 71), 0)
    b_qv = gaussian(arg_keys[4], (2, D), 0.5, 3.0, ((1, 8),))
    w_out = gaussian(arg_keys[5], (D, D), (D // 8) ** -0.5, 0.5, ((0, 2), (1, 4)))
    b_out = gaussian(arg_keys[6], (D,), 0.5, 3.0, ((0, 4),))
    ln2_gain = jnp.clip(1.0 + 0.1 * jax.random.normal(arg_keys[7], (D,), jnp.float32), 0.5, 1.5).astype(jnp.bfloat16)
    ln2_bias = gaussian(arg_keys[8], (D,), 0.5, 3.0, ((0, 4),))
    w_fc1 = gaussian(arg_keys[9], (D, FF), D ** -0.5, 0.1875, ((0, 4), (1, 2)))
    b_fc1 = gaussian(arg_keys[10], (FF,), 0.5, 3.0, ((0, 8),))
    w_fc2 = gaussian(arg_keys[11], (FF, D), FF ** -0.5, 0.09375, ((0, 2), (1, 4)))
    b_fc2 = gaussian(arg_keys[12], (D,), 0.5, 3.0, ((0, 4),))
    cotangent = gaussian(arg_keys[13], (IMAGES, SEQ, D), 1.0, 6.0, ((0, 16),))
    return {"images": images, "ln1_gain": ln1_gain, "ln1_bias": ln1_bias, "w_qkv": w_qkv, "b_qv": b_qv, "w_out": w_out, "b_out": b_out, "ln2_gain": ln2_gain, "ln2_bias": ln2_bias, "w_fc1": w_fc1, "b_fc1": b_fc1, "w_fc2": w_fc2, "b_fc2": b_fc2, "cotangent": cotangent}


epsilon = 1e-06

def matmul(left, right):
    return jnp.dot(left, right, preferred_element_type=jnp.float32)

def widen(value):
    return lax.optimization_barrier(value).astype(jnp.float32)

def norm_forward(hidden_in, norm_gain, norm_bias):
    average = lax.optimization_barrier(jnp.mean(hidden_in, axis=-1, keepdims=True))
    centered = hidden_in - average
    inv_std = lax.rsqrt(lax.optimization_barrier(jnp.mean(centered * centered, axis=-1, keepdims=True)) + epsilon)
    normed = centered * inv_std
    return (normed * norm_gain.astype(jnp.float32) + norm_bias.astype(jnp.float32), normed, inv_std)

def norm_backward(upstream, normed, inv_std, norm_gain):
    scaled = upstream * norm_gain.astype(jnp.float32)
    inner = scaled - lax.optimization_barrier(jnp.mean(scaled, axis=-1, keepdims=True)) - normed * lax.optimization_barrier(jnp.mean(scaled * normed, axis=-1, keepdims=True))
    return (inv_std * inner, lax.optimization_barrier(jnp.sum(upstream * normed, axis=0)), lax.optimization_barrier(jnp.sum(upstream, axis=0)))

def gelu_value(pre_act):
    return 0.5 * pre_act * (1.0 + jax.scipy.special.erf(pre_act * 0.7071067811865476))

def gelu_slope(pre_act):
    cumul = 0.5 * (1.0 + jax.scipy.special.erf(pre_act * 0.7071067811865476))
    density = jnp.exp(-0.5 * pre_act * pre_act) * 0.3989422804014327
    return cumul + pre_act * density

def reference(images, ln1_gain, ln1_bias, w_qkv, b_qv, w_out, b_out, ln2_gain, ln2_bias, w_fc1, b_fc1, w_fc2, b_fc2, cotangent):
    score_scale = HD ** (-0.5)
    params = (ln1_gain, ln1_bias, w_qkv, b_qv, w_out, b_out, ln2_gain, ln2_bias, w_fc1, b_fc1, w_fc2, b_fc2)

    def image_step(totals, pair):
        image, upstream = pair
        resid0 = image.astype(jnp.float32)
        out1, normed1, inv_std1 = norm_forward(resid0, ln1_gain, ln1_bias)
        act1 = out1.astype(jnp.bfloat16)
        queries = ((matmul(act1, w_qkv[0]) + b_qv[0].astype(jnp.float32)) * score_scale).astype(jnp.bfloat16)
        keys_b = matmul(act1, w_qkv[1]).astype(jnp.bfloat16)
        vals_b = (matmul(act1, w_qkv[2]) + b_qv[1].astype(jnp.float32)).astype(jnp.bfloat16)
        query_heads = widen(queries).reshape(SEQ, HEADS, HD)
        key_heads = widen(keys_b).reshape(SEQ, HEADS, HD)
        value_heads = widen(vals_b).reshape(SEQ, HEADS, HD)
        scores = jnp.einsum('qhd,khd->hqk', query_heads, key_heads)
        row_max = lax.optimization_barrier(jnp.max(scores, axis=-1, keepdims=True))
        log_sum = row_max + jnp.log(lax.optimization_barrier(jnp.sum(jnp.exp(scores - row_max), axis=-1, keepdims=True)))
        probs = jnp.exp(scores - log_sum)
        probs_b = probs.astype(jnp.bfloat16)
        context = jnp.einsum('hqk,khd->qhd', widen(probs_b), value_heads).astype(jnp.bfloat16).reshape(SEQ, D)
        resid1 = resid0 + matmul(context, w_out) + b_out.astype(jnp.float32)
        out2, normed2, inv_std2 = norm_forward(resid1, ln2_gain, ln2_bias)
        act2 = out2.astype(jnp.bfloat16)
        pre_act = matmul(act2, w_fc1) + b_fc1.astype(jnp.float32)
        hidden = gelu_value(pre_act).astype(jnp.bfloat16)
        output = resid1 + matmul(hidden, w_fc2) + b_fc2.astype(jnp.float32)
        grad_out = upstream.astype(jnp.float32)
        grad_w_fc2 = matmul(hidden.T, upstream)
        grad_b_fc2 = lax.optimization_barrier(jnp.sum(grad_out, axis=0))
        grad_pre = matmul(upstream, w_fc2.T) * gelu_slope(pre_act)
        grad_pre_b = grad_pre.astype(jnp.bfloat16)
        grad_w_fc1 = matmul(act2.T, grad_pre_b)
        grad_b_fc1 = lax.optimization_barrier(jnp.sum(grad_pre, axis=0))
        grad_act2 = matmul(grad_pre_b, w_fc1.T)
        grad_norm2, grad_ln2_gain, grad_ln2_bias = norm_backward(grad_act2, normed2, inv_std2, ln2_gain)
        grad_resid1 = grad_out + grad_norm2
        grad_resid1_b = grad_resid1.astype(jnp.bfloat16)
        grad_w_out = matmul(context.T, grad_resid1_b)
        grad_b_out = lax.optimization_barrier(jnp.sum(grad_resid1, axis=0))
        grad_context = widen(matmul(grad_resid1_b, w_out.T).astype(jnp.bfloat16)).reshape(SEQ, HEADS, HD)
        grad_vals = jnp.einsum('hqk,qhd->khd', widen(probs_b), grad_context).reshape(SEQ, D)
        grad_probs = jnp.einsum('qhd,khd->hqk', grad_context, value_heads)
        row_dot = lax.optimization_barrier(jnp.sum(probs * grad_probs, axis=-1, keepdims=True))
        grad_scores = widen((probs * (grad_probs - row_dot)).astype(jnp.bfloat16))
        grad_queries = (jnp.einsum('hqk,khd->qhd', grad_scores, key_heads) * score_scale).reshape(SEQ, D)
        grad_keys = jnp.einsum('hqk,qhd->khd', grad_scores, query_heads).reshape(SEQ, D)
        grad_queries_b = grad_queries.astype(jnp.bfloat16)
        grad_keys_b = grad_keys.astype(jnp.bfloat16)
        grad_vals_b = grad_vals.astype(jnp.bfloat16)
        grad_w_qkv = jnp.stack([matmul(act1.T, grad_queries_b), matmul(act1.T, grad_keys_b), matmul(act1.T, grad_vals_b)])
        grad_b_qv = jnp.stack([lax.optimization_barrier(jnp.sum(grad_queries, axis=0)), lax.optimization_barrier(jnp.sum(grad_vals, axis=0))])
        grad_act1 = matmul(grad_queries_b, w_qkv[0].T) + matmul(grad_keys_b, w_qkv[1].T) + matmul(grad_vals_b, w_qkv[2].T)
        grad_norm1, grad_ln1_gain, grad_ln1_bias = norm_backward(grad_act1, normed1, inv_std1, ln1_gain)
        grad_image = grad_resid1 + grad_norm1
        fresh = (grad_ln1_gain, grad_ln1_bias, grad_w_qkv, grad_b_qv, grad_w_out, grad_b_out, grad_ln2_gain, grad_ln2_bias, grad_w_fc1, grad_b_fc1, grad_w_fc2, grad_b_fc2)
        totals = jax.tree.map(lambda before, extra: before + extra, totals, fresh)
        return (totals, (output, grad_image))
    zero_totals = jax.tree.map(lambda weight: jnp.zeros(weight.shape, jnp.float32), params)
    totals, (outputs, grad_images) = lax.scan(image_step, zero_totals, (images, cotangent))
    return (outputs, grad_images, totals[0], totals[1], totals[2], totals[3], totals[4], totals[5], totals[6], totals[7], totals[8], totals[9], totals[10], totals[11])
```

```python
import functools

import jax
import jax.numpy as jnp
from jax import lax
from jax.experimental import pallas as pl
from jax.experimental.pallas import tpu as pltpu
from jax.sharding import PartitionSpec as P

HD = 64
LANES = 128
epsilon = 1e-06
F32 = jnp.float32
BF16 = jnp.bfloat16
VMEM_BYTES = 60 * 2**20

NN = (((1,), (0,)), ((), ()))
NT = (((1,), (1,)), ((), ()))


def dot(left, right, dims=NN):
    return lax.dot_general(left, right, dims, preferred_element_type=F32)


def attention_forward_kernel(tokens, act_ref, w_ref, bias_ref, q_ref, k_ref, v_ref, ctx_ref, lse_ref):
    rows = act_ref.shape[0]
    width = q_ref.shape[1]
    act = act_ref[...]
    q_ref[...] = ((dot(act, w_ref[0]) + bias_ref[0:1, :]) * HD ** (-0.5)).astype(BF16)
    k_ref[...] = dot(act, w_ref[1]).astype(BF16)
    v_ref[...] = (dot(act, w_ref[2]) + bias_ref[1:2, :]).astype(BF16)
    lane = lax.broadcasted_iota(jnp.int32, (rows, LANES), 1)
    whole = tokens // LANES * LANES
    tail_lane = lax.broadcasted_iota(jnp.int32, (rows, rows - whole), 1)
    sums = jnp.zeros((rows, LANES), F32)
    for pair in range(width // LANES):
        columns = slice(pair * LANES, (pair + 1) * LANES)
        queries, keys, vals = q_ref[:, columns], k_ref[:, columns], v_ref[:, columns]
        halves = []
        for side in range(LANES // HD):
            mine = (lane >= side * HD) & (lane < (side + 1) * HD)
            scores = dot(jnp.where(mine, queries, jnp.zeros_like(queries)), keys, NT)
            tail = jnp.where(tail_lane < tokens - whole, scores[:, whole:], -1e30)
            if whole:
                scores = jnp.concatenate([scores[:, :whole], tail], axis=1)
            else:
                scores = tail
            row_max = jnp.max(scores, axis=-1, keepdims=True)
            powers = jnp.exp(scores - row_max)
            total = jnp.sum(powers, axis=-1, keepdims=True)
            probs = (powers * (1.0 / total)).astype(BF16)
            halves.append(dot(probs, vals))
            head = pair * (LANES // HD) + side
            sums = jnp.where(lane == head, row_max + jnp.log(total), sums)
        ctx_ref[:, columns] = jnp.where(lane < HD, halves[0], halves[1]).astype(BF16)
    lse_ref[...] = sums


def attention_forward(tokens, act1, weights, bias):
    rows, _ = act1.shape
    width = weights.shape[2]
    flat = jax.ShapeDtypeStruct((rows, width), BF16)
    flops = 2 * rows * act1.shape[1] * width * 3 + 4 * rows * rows * width
    return pl.pallas_call(
        functools.partial(attention_forward_kernel, tokens),
        out_shape=(flat, flat, flat, flat, jax.ShapeDtypeStruct((rows, LANES), F32)),
        compiler_params=pltpu.CompilerParams(vmem_limit_bytes=VMEM_BYTES),
        cost_estimate=pl.CostEstimate(flops=flops, bytes_accessed=8 * rows * act1.shape[1], transcendentals=rows * rows * width // HD),
        name="attention_forward",
    )(act1, weights, bias)


def attention_backward_kernel(
    tokens, first, gr_ref, grt_ref, actt_ref, q_ref, k_ref, v_ref, ctx_ref, lse_ref, w_ref, wo_ref, *refs
):
    refs = list(refs)
    before_ref = None if first else refs.pop(0)
    gw_ref, gwo_ref, gact_ref, gb_ref = refs
    rows, width = q_ref.shape
    gr = gr_ref[...]
    gwo_ref[0] = dot(grt_ref[...], ctx_ref[...]).astype(BF16)
    grad_context = dot(gr, wo_ref[0]).astype(BF16)
    lane = lax.broadcasted_iota(jnp.int32, (rows, LANES), 1)
    whole = tokens // 16 * 16
    tail_row = lax.broadcasted_iota(jnp.int32, (rows - whole, rows), 0)
    sums = lse_ref[...].T
    dqs, dks, dvs = [], [], []
    for pair in range(width // LANES):
        columns = slice(pair * LANES, (pair + 1) * LANES)
        queries, keys, vals = q_ref[:, columns], k_ref[:, columns], v_ref[:, columns]
        grads = grad_context[:, columns]
        keys_t = keys.astype(F32).T.astype(BF16)
        dq, dk, dv = [], [], []
        for side in range(LANES // HD):
            head = pair * (LANES // HD) + side
            mine = (lane >= side * HD) & (lane < (side + 1) * HD)
            scores = dot(jnp.where(mine, keys, jnp.zeros_like(keys)), queries, NT)
            probs = jnp.exp(scores - sums[head : head + 1, :])
            tail = jnp.where(tail_row < tokens - whole, probs[whole:, :], 0.0)
            probs = jnp.concatenate([probs[:whole, :], tail], axis=0) if whole else tail
            grad_probs = dot(jnp.where(mine, vals, jnp.zeros_like(vals)), grads, NT)
            row_dot = jnp.sum(probs * grad_probs, axis=0, keepdims=True)
            grad_scores = (probs * (grad_probs - row_dot)).astype(BF16)
            dv.append(dot(probs.astype(BF16), grads))
            dk.append(dot(grad_scores, queries))
            dq.append(dot(keys_t[side * HD : (side + 1) * HD, :], grad_scores))
        dqs.append(jnp.concatenate(dq, axis=0).T * HD ** (-0.5))
        dks.append(jnp.where(lane < HD, dk[0], dk[1]))
        dvs.append(jnp.where(lane < HD, dv[0], dv[1]))
    dq, dk, dv = (jnp.concatenate(parts, axis=1) for parts in (dqs, dks, dvs))
    gb_ref[0:1, :] = jnp.sum(dq, axis=0, keepdims=True)
    gb_ref[1:2, :] = jnp.sum(dv, axis=0, keepdims=True)
    total = None if first else before_ref[...]
    for which, grad in enumerate((dq, dk, dv)):
        grad = grad.astype(BF16)
        gw_ref[which] = dot(actt_ref[...], grad).astype(BF16)
        term = dot(grad, w_ref[which], NT)
        total = term if total is None else total + term
    gact_ref[...] = total


def attention_backward(tokens, gr, gr_t, act1_t, saved, weights, out_weight, before):
    rows, depth = gr.shape
    width = weights.shape[2]
    operands = (gr, gr_t, act1_t, *saved, weights, out_weight) + (() if before is None else (before,))
    flops = 2 * rows * depth * width * 8 + 10 * rows * rows * width
    return pl.pallas_call(
        functools.partial(attention_backward_kernel, tokens, before is None),
        out_shape=(
            jax.ShapeDtypeStruct((3, depth, width), BF16),
            jax.ShapeDtypeStruct((1, depth, width), BF16),
            jax.ShapeDtypeStruct((rows, depth), F32),
            jax.ShapeDtypeStruct((2, width), F32),
        ),
        compiler_params=pltpu.CompilerParams(vmem_limit_bytes=VMEM_BYTES),
        cost_estimate=pl.CostEstimate(flops=flops, bytes_accessed=24 * rows * depth, transcendentals=rows * rows * width // HD),
        name="attention_backward",
    )(*operands)


def feed_forward_kernel(act_ref, cot_ref, w_ref, bias_ref, hid_ref, gp_ref, mlp_ref, gact_ref, gb_ref, mlp_acc, gact_acc):
    step = pl.program_id(0)
    w1, w2 = w_ref[0, 0], w_ref[0, 1]
    pre = dot(act_ref[...], w1) + bias_ref[0]
    back = dot(cot_ref[...], w2)
    cumul = 0.5 * (1.0 + lax.erf(pre * 0.7071067811865476))
    density = jnp.exp(-0.5 * pre * pre) * 0.3989422804014327
    hidden = (pre * cumul).astype(BF16)
    grad_pre = back * (cumul + pre * density)
    gb_ref[0] = jnp.sum(grad_pre, axis=0, keepdims=True)
    grad_pre = grad_pre.astype(BF16)
    hid_ref[0] = hidden
    gp_ref[0] = grad_pre
    mlp = dot(hidden, w2, NT)
    gact = dot(grad_pre, w1, NT)

    @pl.when(step == 0)
    def _():
        mlp_acc[...] = mlp
        gact_acc[...] = gact

    @pl.when(step > 0)
    def _():
        mlp_acc[...] += mlp
        gact_acc[...] += gact

    @pl.when(step == pl.num_programs(0) - 1)
    def _():
        mlp_ref[...] = mlp_acc[...].astype(mlp_ref.dtype)
        gact_ref[...] = gact_acc[...].astype(gact_ref.dtype)


def feed_forward(act2, cot, weights, bias, out_dtype):
    rows, depth = act2.shape
    slots, _, _, width = weights.shape
    whole = pl.BlockSpec((rows, depth), lambda s: (0, 0))
    block = pl.BlockSpec((1, rows, width), lambda s: (s, 0, 0))
    line = pl.BlockSpec((1, 1, width), lambda s: (s, 0, 0))
    hidden = jax.ShapeDtypeStruct((slots, rows, width), BF16)
    total = jax.ShapeDtypeStruct((rows, depth), out_dtype)
    return pl.pallas_call(
        feed_forward_kernel,
        grid=(slots,),
        in_specs=[whole, whole, pl.BlockSpec((1, 2, depth, width), lambda s: (s, 0, 0, 0)), line],
        out_specs=(block, block, whole, whole, line),
        out_shape=(hidden, hidden, total, total, jax.ShapeDtypeStruct((slots, 1, width), F32)),
        scratch_shapes=[pltpu.VMEM((rows, depth), F32)] * 2,
        compiler_params=pltpu.CompilerParams(vmem_limit_bytes=VMEM_BYTES),
        cost_estimate=pl.CostEstimate(
            flops=8 * rows * depth * width * slots, bytes_accessed=4 * slots * width * (depth + rows), transcendentals=2 * rows * width * slots
        ),
        name="feed_forward",
    )(act2, cot, weights, bias)


def weight_gradient_kernel(count, *refs):
    acts, cots = refs[:count], refs[count : 2 * count]
    gps, hids = refs[2 * count : 3 * count], refs[3 * count : 4 * count]
    out_ref = refs[4 * count]
    first = second = None
    for act, cot, gp, hid in zip(acts, cots, gps, hids):
        one, two = dot(act[...], gp[0]), dot(cot[...], hid[0])
        first = one if first is None else first + one
        second = two if second is None else second + two
    out_ref[0, 0] = first.astype(BF16)
    out_ref[0, 1] = second.astype(BF16)


def weight_gradients(acts_t, cots_t, gps, hids):
    count = len(acts_t)
    depth, rows = acts_t[0].shape
    slots, _, width = gps[0].shape
    whole = pl.BlockSpec((depth, rows), lambda s: (0, 0))
    block = pl.BlockSpec((1, rows, width), lambda s: (s, 0, 0))
    return pl.pallas_call(
        functools.partial(weight_gradient_kernel, count),
        grid=(slots,),
        in_specs=[whole] * (2 * count) + [block] * (2 * count),
        out_specs=pl.BlockSpec((1, 2, depth, width), lambda s: (s, 0, 0, 0)),
        out_shape=jax.ShapeDtypeStruct((slots, 2, depth, width), BF16),
        compiler_params=pltpu.CompilerParams(vmem_limit_bytes=VMEM_BYTES),
        cost_estimate=pl.CostEstimate(
            flops=4 * count * rows * depth * width * slots, bytes_accessed=4 * slots * width * (depth + count * rows), transcendentals=0
        ),
        name="weight_gradients",
    )(*acts_t, *cots_t, *gps, *hids)


def add(left, right):
    return (left.astype(F32) + right.astype(F32)).astype(BF16)


def after(value, *others):
    return lax.optimization_barrier((value, *others))[0]


def norm_forward(hidden_in, norm_gain, norm_bias):
    average = jnp.mean(hidden_in, axis=-1, keepdims=True)
    centered = hidden_in - average
    inv_std = lax.rsqrt(jnp.mean(centered * centered, axis=-1, keepdims=True) + epsilon)
    normed = centered * inv_std
    return normed * norm_gain + norm_bias, normed, inv_std


def norm_backward(upstream, normed, inv_std, norm_gain):
    scaled = upstream * norm_gain
    inner = scaled - jnp.mean(scaled, axis=-1, keepdims=True) - normed * jnp.mean(scaled * normed, axis=-1, keepdims=True)
    return inv_std * inner, jnp.sum(upstream * normed, axis=0), jnp.sum(upstream, axis=0)


def make_body(reps, shards, splits):
    if splits != 2 or reps & (reps - 1) or reps < 2:
        raise ValueError("unsupported mesh")
    strides = []
    stride = reps // 2
    while stride:
        strides.append(stride)
        stride //= 2
    far, near = strides[:-1], strides[-1]
    order = [0]
    for stride in strides:
        order = order + [slot ^ stride for slot in order]
    place = [order.index(slot) for slot in range(reps)]

    def swap_rep(value, stride):
        return lax.ppermute(value, "rep", [(i, i ^ stride) for i in range(reps)])

    def swap_tp(value):
        return lax.ppermute(value, "tp", [(0, 1), (1, 0)])

    def fetch(value, distance):
        return lax.ppermute(value, "fsdp", [(i, (i - distance) % shards) for i in range(shards)])

    def deliver(value, distance):
        return lax.ppermute(value, "fsdp", [(i, (i + distance) % shards) for i in range(shards)])

    def gather_shards(piece):
        return jnp.concatenate([piece] + [fetch(piece, d) for d in range(1, shards)], axis=1)

    def spread(value):
        for stride in far:
            value = jnp.concatenate([value, swap_rep(value, stride)], axis=2)
        return value

    def gather_heads(piece):
        mine = gather_shards(piece)
        other = swap_tp(mine)
        mine, other = spread(mine), spread(other)
        return mine, swap_rep(mine, near), other, swap_rep(other, near)

    def gather_hidden(piece):
        value = gather_shards(piece)[None]
        for stride in strides:
            value = jnp.concatenate([value, swap_rep(value, stride)], axis=0)
        return value

    def scatter_shards(value):
        block = value.shape[1] // shards
        total = value[:, :block].astype(F32)
        for d in range(1, shards):
            total = total + deliver(value[:, d * block : (d + 1) * block], d).astype(F32)
        return total.astype(BF16)

    def collect(value, rep, axis):
        for bit, stride in enumerate(reversed(strides)):
            partner = swap_rep(value, stride)
            low = (rep // stride) % 2 == 0
            value = jnp.concatenate([jnp.where(low, value, partner), jnp.where(low, partner, value)], axis=axis)
        return value

    def reduce_far(value):
        for stride in reversed(far):
            half = value.shape[2] // 2
            value = add(value[:, :, :half], swap_rep(value[:, :, half:], stride))
        return value

    def relative(vector, rep):
        blocks = vector.reshape(vector.shape[:-1] + (reps, -1))
        picked = [lax.dynamic_index_in_dim(blocks, rep ^ slot, blocks.ndim - 2, keepdims=False) for slot in order]
        return jnp.concatenate(picked, axis=-1)

    def absolute(vector, rep):
        blocks = vector.reshape(vector.shape[:-1] + (reps, -1))
        blocks = jnp.stack([blocks[..., slot, :] for slot in place], axis=-2)
        picked = [lax.dynamic_index_in_dim(blocks, rep ^ slot, blocks.ndim - 2, keepdims=False) for slot in range(reps)]
        return jnp.concatenate(picked, axis=-1)

    def body(images, ln1_gain, ln1_bias, w_qkv, b_qv, w_out, b_out, ln2_gain, ln2_bias, w_fc1, b_fc1, w_fc2, b_fc2, cotangent):
        batch, tokens, depth = images.shape
        if batch != splits:
            raise ValueError("unsupported batch")
        rows = -(-tokens // 16) * 16
        block = depth // shards
        rep, shard, split = lax.axis_index("rep"), lax.axis_index("fsdp"), lax.axis_index("tp")
        heads, hiddens = w_qkv.shape[2], w_fc1.shape[1]
        head_w, hidden_w = heads // reps, hiddens // reps

        def roll(value, blocks):
            axis = value.ndim - 1
            twice = jnp.concatenate([value, value], axis=axis)
            return lax.dynamic_slice_in_dim(twice, blocks * block, depth, axis)

        def roll_in(value):
            return roll(value, shard)

        def roll_out(value):
            return roll(value, (shards - shard) % shards)

        qkv_piece = lax.dynamic_slice_in_dim(w_qkv, rep * head_w, head_w, 2)
        out_piece = lax.dynamic_slice_in_dim(w_out, rep * head_w, head_w, 0).T[None]
        fc1_piece = lax.dynamic_slice_in_dim(w_fc1, rep * hidden_w, hidden_w, 1)
        fc2_piece = lax.dynamic_slice_in_dim(w_fc2, rep * hidden_w, hidden_w, 0).T
        fc_piece = jnp.stack([fc1_piece, fc2_piece])
        qkv_groups = gather_heads(qkv_piece)
        out_groups = gather_heads(after(out_piece, qkv_groups[0]))
        fc_full = gather_hidden(after(fc_piece, qkv_groups[0]))

        wides = (ln1_gain, ln1_bias, b_out, ln2_gain, ln2_bias, b_fc2)
        packed = jnp.concatenate([*wides, b_qv.reshape(-1), b_fc1])
        gathered = lax.all_gather(packed, ("tp", "fsdp"), axis=0).reshape(splits, shards, -1)
        mid = len(wides) * block
        end = mid + b_qv.size
        wide = gathered[0, :, :mid].reshape(shards, len(wides), block).transpose(1, 0, 2).reshape(len(wides), depth)
        gain1, bias1, bias_out, gain2, bias2, bias_fc2 = roll_in(wide).astype(F32)[:, None, :]
        bias_qv = gathered[:, :, mid:end].reshape(splits, shards, 2, -1).transpose(0, 2, 1, 3).reshape(splits, 2, heads)
        bias_qv = relative(bias_qv.astype(F32), rep)
        bias_qv = [lax.dynamic_index_in_dim(bias_qv, i, 0, keepdims=False) for i in (split, 1 - split)]
        half = heads // 2
        bias_groups = [part for pair in bias_qv for part in (pair[:, :half], pair[:, half:])]
        bias_fc1 = gathered[:, :, end:].reshape(splits, hiddens)
        bias_fc1 = lax.dynamic_index_in_dim(bias_fc1, split, 0, keepdims=False)
        bias_fc1 = relative(bias_fc1.astype(F32), rep).reshape(reps, 1, hidden_w)

        def pick(value, i):
            image = lax.dynamic_index_in_dim(value, i, 0, keepdims=False)
            return jnp.pad(roll_in(image), ((0, rows - tokens), (0, 0)))

        resid0 = pick(images, split).astype(F32)
        cot = pick(cotangent, split)
        cot_other = pick(cotangent, 1 - split)
        out_one, normed1, inv_std1 = norm_forward(resid0, gain1, bias1)
        act1 = out_one.astype(BF16)
        act1_t = act1.T
        saved = [attention_forward(tokens, act1, w, b) for w, b in zip(qkv_groups, bias_groups)]
        context = jnp.concatenate([group[3] for group in saved], axis=1)
        out_full = jnp.concatenate([w[0] for w in out_groups], axis=1)
        resid1 = resid0 + dot(context, out_full, NT) + bias_out
        out_two, normed2, inv_std2 = norm_forward(resid1, gain2, bias2)
        act2 = out_two.astype(BF16)
        act2_other = swap_tp(act2)

        hid, gp, mlp, gact2, gb1 = feed_forward(act2, cot, fc_full, bias_fc1, F32)
        hid_o, gp_o, mlp_o, gact2_o, gb1_o = feed_forward(act2_other, cot_other, fc_full, bias_fc1, BF16)
        grad_act2 = gact2 + swap_tp(gact2_o).astype(F32)
        grad_fc = weight_gradients((act2.T, act2_other.T), (cot.T, cot_other.T), (gp, gp_o), (hid, hid_o))
        mlp_in = swap_tp(after(mlp_o, grad_act2))
        output = (resid1 + mlp + mlp_in.astype(F32) + bias_fc2).astype(BF16)
        output_o = swap_tp(output)

        grad_out = cot.astype(F32)
        grad_b_fc2 = jnp.sum(grad_out, axis=0)
        grad_norm2, grad_ln2_gain, grad_ln2_bias = norm_backward(grad_act2, normed2, inv_std2, gain2)
        grad_resid1 = grad_out + grad_norm2
        grad_b_out = jnp.sum(grad_resid1, axis=0)
        gr = grad_resid1.astype(BF16)
        gr_t = gr.T

        keep = reps // 2
        grad_fc = add(grad_fc[:keep], swap_rep(grad_fc[keep:], near))
        for stride in reversed(far):
            n = grad_fc.shape[0] // 2
            grad_fc = add(grad_fc[:n], swap_rep(grad_fc[n:], stride))
        grad_fc = scatter_shards(grad_fc[0])
        grad_fc = collect(grad_fc, rep, 2)
        grad_w_fc1 = grad_fc[0].astype(F32)
        grad_w_fc2 = grad_fc[1].T.astype(F32)

        results = [None] * 4
        grad_act1 = None
        for i in (3, 2, 1, 0):
            results[i] = attention_backward(tokens, gr, gr_t, act1_t, saved[i], qkv_groups[i], out_groups[i], grad_act1)
            grad_act1 = results[i][2]

        def owned(which):
            mine, mine_far, other, other_far = (result[which] for result in results)
            other = reduce_far(add(other, swap_rep(other_far, near)))
            mine = reduce_far(add(mine, swap_rep(mine_far, near)))
            mine = add(mine, swap_tp(other))
            return collect(scatter_shards(mine), rep, 2).astype(F32)

        grad_w_out = owned(1)[0].T
        grad_w_qkv = owned(0)

        grad_norm1, grad_ln1_gain, grad_ln1_bias = norm_backward(grad_act1, normed1, inv_std1, gain1)
        grad_image = (grad_resid1 + grad_norm1).astype(BF16)
        grad_image_o = swap_tp(grad_image)

        wide_grads = roll_out(jnp.stack([grad_ln1_gain, grad_ln1_bias, grad_b_out, grad_ln2_gain, grad_ln2_bias, grad_b_fc2]))
        grad_qv = [result[3] for result in results]
        grad_qv = [absolute(jnp.concatenate(grad_qv[i : i + 2], axis=1), rep) for i in (0, 2)]
        first_half = split == 0
        grad_qv = jnp.stack([jnp.where(first_half, grad_qv[0], grad_qv[1]), jnp.where(first_half, grad_qv[1], grad_qv[0])])
        grad_b1 = absolute((gb1 + gb1_o).reshape(-1), rep)
        grad_b1 = jnp.stack([jnp.where(first_half, grad_b1, 0.0), jnp.where(first_half, 0.0, grad_b1)])
        small = jnp.concatenate([wide_grads.reshape(-1), grad_qv.reshape(-1), grad_b1.reshape(-1)])
        small = lax.psum(small, ("rep", "fsdp", "tp"))
        wide_end = len(wides) * depth
        qv_end = wide_end + splits * 2 * heads
        wide_grads = lax.dynamic_slice_in_dim(small[:wide_end].reshape(len(wides), depth), shard * block, block, 1)
        qv = lax.dynamic_index_in_dim(small[wide_end:qv_end].reshape(splits, 2, heads), split, 0, keepdims=False)
        qv = lax.dynamic_slice_in_dim(qv, shard * (heads // shards), heads // shards, 1)
        b1 = lax.dynamic_index_in_dim(small[qv_end:].reshape(splits, hiddens), split, 0, keepdims=False)
        b1 = lax.dynamic_slice_in_dim(b1, shard * (hiddens // shards), hiddens // shards, 0)

        def both(mine, other):
            mine, other = roll_out(mine[:tokens]).astype(F32), roll_out(other[:tokens]).astype(F32)
            return jnp.stack([jnp.where(first_half, mine, other), jnp.where(first_half, other, mine)])

        return (
            both(output, output_o),
            both(grad_image, grad_image_o),
            wide_grads[0],
            wide_grads[1],
            grad_w_qkv,
            qv,
            grad_w_out,
            wide_grads[2],
            wide_grads[3],
            wide_grads[4],
            grad_w_fc1,
            b1,
            grad_w_fc2,
            wide_grads[5],
        )

    return body


def solution(mesh):
    token = P(("rep", "fsdp"), None, None)
    wide = P("fsdp")
    heads = P(None, "fsdp", "tp")
    heads_bias = P(None, ("tp", "fsdp"))
    across = P("tp", "fsdp")
    hidden_bias = P(("tp", "fsdp"))
    weights = (wide, wide, heads, heads_bias, across, wide, wide, wide, P("fsdp", "tp"), hidden_bias, across, wide)
    body = make_body(mesh.shape["rep"], mesh.shape["fsdp"], mesh.shape["tp"])
    return jax.shard_map(
        body, mesh=mesh, in_specs=(token, *weights, token), out_specs=(token, token, *weights), check_vma=False
    )
```
